32 devices in a mesh: expert: 8 (over z, y), replica: 4 (over x, core).
Axes of the slice: x: 2, y: 2, z: 4, core: 2. Of those that a mesh axis runs over, the one named last changes fastest.
Arguments:
- tokens: bfloat16 [2048, 2880], P(('expert', 'replica')), may hold values from -6 to 6
- expert_ids: int32 [2048, 4], P(('expert', 'replica')), may hold values from 0 to 7, all different within a row; in each aligned block of 64 rows (0 to 63, 64 to 127, ...) at most 48 rows name the same one
- gate_codes: int32 [2048, 4], P(('expert', 'replica')), may hold values from 1 to 65535
- w_gate: bfloat16 [8, 2880, 2880], P('expert', None, 'replica'), may hold values from -0.109375 to 0.109375
- w_up: bfloat16 [8, 2880, 2880], P('expert', None, 'replica'), may hold values from -0.109375 to 0.109375
- w_down: bfloat16 [8, 2880, 2880], P('expert', 'replica'), may hold values from -0.109375 to 0.109375
Outputs:
- mixed: bfloat16 [2048, 2880], P(('expert', 'replica'))
The draws below stay inside these ranges and needn't reach their ends.
Inputs may be any that keep to these rules, and one draw needn't show every extreme that they name: `expert_ids`: each row names 4 different experts. Among the 64 rows of one device each expert is named at most 48 times, a bound that some block reaches.
All inputs are finite; a program needn't handle non-finite values.
Results may differ from the reference program's by a relative error of at most 0.015.
Values may be sent and summed in bfloat16 or wider, within the bound.
A program may use at most 128 MiB of HBM per device.

```python
import math
import jax
import jax.numpy as jnp
import numpy as np
from jax import lax

D = 2880
FF = 2880
TOP = 4
TOK_DEV = 64
EXPERTS = 8
CAP = 48
TOKENS = 2048
N_EXPERT = 8
N_REPLICA = 4


def with_ends(entries, stream_key, smallest, largest):
    index_at = [jax.random.randint(jax.random.fold_in(stream_key, axis), (), 0, length) for axis, length in enumerate(entries.shape)]
    longest = entries.shape.index(max(entries.shape))
    next_to = index_at[:longest] + [(index_at[longest] + 1) % entries.shape[longest]] + index_at[longest + 1:]
    return entries.at[tuple(index_at)].set(smallest).at[tuple(next_to)].set(largest)


def block_levels(key, extent, shards, low, top_value):
    level, own = 1.0, jax.random.fold_in(key, 6)
    for position, blocks in shards:
        draws = jnp.exp(jax.random.uniform(jax.random.fold_in(own, position), (blocks,), jnp.float32, low / len(shards), top_value / len(shards)))
        level = level * jnp.repeat(draws, extent[position] // blocks).reshape([-1 if axis == position else 1 for axis in range(len(extent))])
    return level


def deal_out(stream_key, own, number, rows, number_of, top, reach, lean):
    order = jax.random.permutation(stream_key, number_of)
    crowded, usual = shares(number_of, rows * top, reach, lean, True), shares(number_of, rows * top, reach, lean, False)
    places = jnp.arange(number_of)

    def named(sizes, turn):
        used = int((sizes > 0).sum())
        fixed = max(1, used // 4)
        passed = fixed + (places - fixed + turn * (used - fixed)) % max(1, number_of - fixed)
        return jnp.zeros((number_of,), jnp.int32).at[order[jnp.where(places < fixed, places, passed)]].set(jnp.asarray(sizes, jnp.int32))

    sizes = jnp.where(number % 4 == 0, named(crowded, number // 4), named(usual, number - number // 4 - 1))
    mixed = jax.random.permutation(jax.random.fold_in(own, 3), number_of)
    donor, receiver = mixed[0:number_of // 2 * 2:2], mixed[1:number_of // 2 * 2:2]
    margin = jnp.minimum(sizes[donor] - 1, reach - sizes[receiver]) // 2
    margin = jnp.where((donor == order[0]) | (receiver == order[0]) | (sizes[receiver] == 0), 0, jnp.maximum(margin, 0))
    passed = jax.random.randint(jax.random.fold_in(own, 4), (number_of // 2,), 0, 1 << 20) % (margin + 1)
    sizes = sizes.at[donor].add(-passed).at[receiver].add(passed)
    items = jnp.searchsorted(jnp.cumsum(sizes), jnp.arange(rows * top), side="right").astype(jnp.int32)
    listing = items.reshape(top, rows).T
    listing = listing[jax.random.permutation(jax.random.fold_in(own, 1), rows)]
    turn = jax.random.randint(jax.random.fold_in(own, 2), (rows, 1), 0, top)
    return jnp.take_along_axis(listing, (jnp.arange(top)[None, :] + turn) % top, axis=1)


def shares(amount, total, reach, slope, full):
    loads = [(1 << 20) // math.isqrt(standing ** slope) + 1 for standing in range(1, amount + 1)]
    largest = reach if full else min(reach, max(-(-total // amount), total * loads[0] // sum(loads)))
    least = 1 if total - largest >= amount - 1 else 0
    given, spare = [largest] + [least] * (amount - 1), total - largest - least * (amount - 1)
    while spare > 0:
        free = [i for i in range(1, amount) if given[i] < largest] or [i for i in range(1, amount) if given[i] < reach]
        whole, remaining = sum([loads[i] for i in free]), spare
        for i in free:
            addition = min(reach - given[i], max(1, remaining * loads[i] // whole), spare)
            given[i] = given[i] + addition
            spare = spare - addition
    return np.array(given)


def centred(stream_key, extent, width, reach, pieces=(), held_as=jnp.bfloat16):
    array = width * jax.random.normal(stream_key, extent, jnp.float32)
    if pieces:
        array = array * block_levels(stream_key, extent, pieces, -0.22, 0.18)
    return jnp.clip(array, -reach, reach).astype(held_as)


def setup_inputs(seed: int = 0) -> dict:
    arg_keys = jax.random.split(jax.random.key(seed), 7)
    tokens = centred(arg_keys[0], (TOKENS, D), 1.0, 6.0, ((0, 32),))
    expert_ids_keys = jax.random.split(jax.random.fold_in(arg_keys[1], 1), TOKENS // TOK_DEV)
    expert_ids_turns = jax.random.permutation(jax.random.fold_in(arg_keys[1], 3), TOKENS // TOK_DEV)
    expert_ids = jax.vmap(lambda own, number: deal_out(jax.random.fold_in(arg_keys[1], 2), own, number, TOK_DEV, EXPERTS, TOP, CAP, 2))(expert_ids_keys, expert_ids_turns).reshape((TOKENS, TOP))
    gate_codes = with_ends(jax.random.randint(arg_keys[2], (TOKENS, TOP), 1, 65536), jax.random.fold_in(arg_keys[2], 1), 1, 65535).astype(jnp.int32)
    w_gate = centred(arg_keys[3], (EXPERTS, D, FF), D ** -0.5, 0.109375, ((0, 8), (2, 4)))
    w_up = centred(arg_keys[4], (EXPERTS, D, FF), D ** -0.5, 0.109375, ((0, 8), (2, 4)))
    w_down = centred(arg_keys[5], (EXPERTS, FF, D), FF ** -0.5, 0.109375, ((0, 8), (1, 4)))
    return {"tokens": tokens, "expert_ids": expert_ids, "gate_codes": gate_codes, "w_gate": w_gate, "w_up": w_up, "w_down": w_down}


def activate(gate, up):
    return gate * jax.nn.sigmoid(1.702 * gate) * (up + 1.0)


def reference(tokens, expert_ids, gate_codes, w_gate, w_up, w_down):
    count_rows = tokens.shape[0]
    flat_ids = expert_ids.reshape(-1)
    gates = gate_codes.reshape(-1).astype(jnp.float32) / 65536.0
    most_rows = N_EXPERT * N_REPLICA * CAP
    part_width = FF // N_REPLICA

    def one_expert(expert, total):
        chosen = flat_ids == expert
        count = jnp.sum(chosen.astype(jnp.int32))
        where = jnp.nonzero(chosen, size=most_rows, fill_value=0)[0].astype(jnp.int32)
        valid = (jnp.arange(most_rows, dtype=jnp.int32) < count).astype(jnp.float32)
        owner = (where // TOP).astype(jnp.int32)
        rows = tokens[owner]
        gate = jnp.dot(rows, w_gate[expert], preferred_element_type=jnp.float32)
        up = jnp.dot(rows, w_up[expert], preferred_element_type=jnp.float32)
        hidden = activate(gate, up).astype(jnp.bfloat16)
        result = jnp.zeros((most_rows, D), jnp.float32)
        for part in range(N_REPLICA):
            piece = jnp.dot(hidden[:, part * part_width:(part + 1) * part_width],
                            w_down[expert, part * part_width:(part + 1) * part_width],
                            preferred_element_type=jnp.float32).astype(jnp.bfloat16)
            piece = lax.optimization_barrier(piece)
            result = result + piece.astype(jnp.float32)
        rounded = lax.optimization_barrier(result.astype(jnp.bfloat16))
        weight = gates[where] * valid
        return total.at[owner].add(rounded.astype(jnp.float32) * weight[:, None])

    total = lax.fori_loop(0, EXPERTS, one_expert, jnp.zeros((count_rows, D), jnp.float32))
    return total.astype(jnp.bfloat16)
```

```python
import functools

import jax
import jax.numpy as jnp
from jax import lax
from jax.experimental import pallas as pl
from jax.experimental.pallas import tpu as pltpu
from jax.sharding import PartitionSpec as P

MESH = pl.DeviceIdType.MESH
CORES = 2
LANES = 128


def activate(gate, up):
    return gate * jax.nn.sigmoid(1.702 * gate) * (up + 1.0)


def spans(extent, step):
    return [(low, min(low + step, extent)) for low in range(0, extent, step)]


def fused(
    depth, experts, cap, tokens, meta, w_gate, w_up, w_down, out,
    tok_buf, meta_buf, y_out, x_buf, wg, wu, wd, hid, part, c_in, x_out, x_in,
    mine, y_in, z_out, z_in, acc, w_sem,
    zt_s, zt_r, zm_s, zm_r, y_s, y_r, x_s, x_r, c_s, c_r,
    pc_s, pc_r, px_s, px_r, py_s, py_r, pz_s, pz_r,
):
    rows, width = tokens.shape
    f32, bf16 = jnp.float32, jnp.bfloat16
    expert, replica = lax.axis_index("expert"), lax.axis_index("replica")
    z, y = expert // 2, expert % 2
    other = z * 2 + (1 - y)
    y_peer = {"expert": other}
    x_peer = {"replica": (replica + CORES) % (2 * CORES)}
    c_peer = {"replica": replica // CORES * CORES + (1 - replica % CORES)}

    def z_peer(back):
        return {"expert": ((z + depth - back) % depth) * 2 + y}

    def z_ahead(ahead):
        return {"expert": ((z + ahead) % depth) * 2 + y}

    def send(src, dst, ssem, rsem, peer):
        pltpu.make_async_remote_copy(
            src_ref=src, dst_ref=dst, send_sem=ssem, recv_sem=rsem,
            device_id=peer, device_id_type=MESH,
        ).start()

    def arrived(dst, sem):
        pltpu.make_async_copy(dst, dst, sem).wait()

    barrier = pltpu.get_barrier_semaphore()
    for peer in [z_peer(s) for s in range(1, depth)] + [y_peer, x_peer, c_peer]:
        pl.semaphore_signal(barrier, inc=1, device_id=peer, device_id_type=MESH)
    pl.semaphore_wait(barrier, depth + 2)

    for s in range(1, depth):
        send(meta, meta_buf.at[s], zm_s.at[s], zm_r.at[s], z_peer(s))
        send(tokens, tok_buf.at[s], zt_s.at[s], zt_r.at[s], z_peer(s))
    pltpu.make_async_copy(meta, meta_buf.at[0], zm_r.at[0]).start()
    pltpu.make_async_copy(tokens, tok_buf.at[0], zt_r.at[0]).start()
    loads = [
        pltpu.make_async_copy(src.at[0], dst, w_sem.at[i])
        for i, (src, dst) in enumerate(((w_gate, wg), (w_up, wu), (w_down, wd)))
    ]
    for load in loads:
        load.start()

    group = 2 * cap

    def pick(s, which):
        ranks = meta_buf[s, pl.ds(rows, 2 * experts), :]
        sub = lax.broadcasted_iota(jnp.int32, ranks.shape, 0)
        rank = jnp.sum(jnp.where(sub == which, ranks, 0.0), axis=0, keepdims=True)[:, :rows]
        slot = lax.broadcasted_iota(jnp.int32, (cap, rows), 0).astype(f32)
        return jnp.where(slot == rank, 1.0, 0.0).astype(bf16)

    def spread(s, which):
        ranks = meta_buf[s, pl.ds(0, rows), :]
        lane = lax.broadcasted_iota(jnp.int32, ranks.shape, 1)
        rank = jnp.sum(jnp.where(lane == which, ranks, 0.0), axis=1, keepdims=True)
        weight = jnp.sum(jnp.where(lane == which + experts, ranks, 0.0), axis=1, keepdims=True)
        slot = lax.broadcasted_iota(jnp.int32, (rows, cap), 1).astype(f32)
        return jnp.where(slot == rank, 1.0, 0.0).astype(bf16), weight

    def choose(s):
        arrived(meta_buf.at[s], zm_r.at[s])
        arrived(tok_buf.at[s], zt_r.at[s])
        block = tok_buf[s]
        y_out[s] = jnp.dot(pick(s, other), block, preferred_element_type=f32).astype(bf16)
        send(y_out.at[s], x_buf.at[s, pl.ds(cap, cap)], y_s.at[s], y_r.at[s], y_peer)
        x_buf[s, pl.ds(0, cap), :] = jnp.dot(
            pick(s, expert), block, preferred_element_type=f32
        ).astype(bf16)

    def to_x(s):
        arrived(y_out.at[s], y_r.at[s])
        send(x_buf.at[s, pl.ds(0, group)], x_buf.at[s, pl.ds(group, group)],
             x_s.at[s], x_r.at[s], x_peer)

    def to_core(s):
        arrived(x_in.at[s], x_r.at[s])
        send(x_buf.at[s, pl.ds(0, 2 * group)], x_buf.at[s, pl.ds(2 * group, 2 * group)],
             c_s.at[s], c_r.at[s], c_peer)

    def ffn(s):
        arrived(c_in.at[s], c_r.at[s])

        @pl.when(s == 0)
        def _():
            for load in loads:
                load.wait()

        for low, high in spans(wg.shape[1], 256):
            block = x_buf[s]
            gate = jnp.dot(block, wg[:, low:high], preferred_element_type=f32)
            up = jnp.dot(block, wu[:, low:high], preferred_element_type=f32)
            hid[:, low:high] = activate(gate, up).astype(bf16)
        for low, high in spans(width, 512):
            part[s, :, low:high] = jnp.dot(
                hid[...], wd[:, low:high], preferred_element_type=f32
            ).astype(bf16)
        send(part.at[s, pl.ds(2 * group, 2 * group)], c_in.at[s], pc_s.at[s], pc_r.at[s], c_peer)

    def sum_core(s):
        arrived(c_in.at[s], pc_r.at[s])
        x_out[s] = (
            part[s, pl.ds(group, group), :].astype(f32) + c_in[s, pl.ds(group, group), :].astype(f32)
        ).astype(bf16)
        send(x_out.at[s], x_in.at[s], px_s.at[s], px_r.at[s], x_peer)

    def sum_x(s):
        arrived(x_in.at[s], px_r.at[s])
        mine[s] = (
            part[s, pl.ds(0, group), :].astype(f32)
            + c_in[s, pl.ds(0, group), :].astype(f32)
            + x_in[s].astype(f32)
        ).astype(bf16)
        send(mine.at[s, pl.ds(cap, cap)], y_in.at[s], py_s.at[s], py_r.at[s], y_peer)

    def combine(s):
        arrived(y_in.at[s], py_r.at[s])
        own_spread, own_weight = spread(s, expert)
        far_spread, far_weight = spread(s, other)
        total = own_weight * jnp.dot(
            own_spread, mine[s, pl.ds(0, cap), :], preferred_element_type=f32
        ) + far_weight * jnp.dot(far_spread, y_in[s], preferred_element_type=f32)

        @pl.when(s == 0)
        def _():
            acc[...] = total

        @pl.when(s > 0)
        def _():
            z_out[s] = total.astype(bf16)
            send(z_out.at[s], z_in.at[s], pz_s.at[s], pz_r.at[s], z_ahead(s))

    steps = ((choose, 0), (to_core, 1), (to_x, 0), (ffn, 2), (sum_core, 3), (sum_x, 4), (combine, 5))

    def tick(t, carry):
        for step, lag in steps:
            @pl.when((t >= lag) & (t < depth + lag))
            def _():
                step(t - lag)
        return carry

    lax.fori_loop(0, depth + steps[-1][1], tick, 0)

    total = acc[...]
    for s in range(1, depth):
        arrived(z_in.at[s], pz_r.at[s])
        total = total + z_in[s].astype(f32)
    out[...] = total.astype(bf16)
    for s in range(depth):
        if s:
            arrived(meta_buf.at[s], zm_s.at[s])
            arrived(tok_buf.at[s], zt_s.at[s])
            arrived(z_out.at[s], pz_s.at[s])
        arrived(y_out.at[s], y_s.at[s])
        arrived(x_in.at[s], x_s.at[s])
        arrived(c_in.at[s], c_s.at[s])
        arrived(c_in.at[s], pc_s.at[s])
        arrived(x_out.at[s], px_s.at[s])
        arrived(y_in.at[s], py_s.at[s])


def gathered_plan(tokens, expert_ids, gate_codes, w_gate, w_up, w_down, capacity, expert_count):
    rows, top = expert_ids.shape
    width = tokens.shape[1]
    part_width = w_gate.shape[2]
    depth = lax.axis_size("expert") // 2
    f32, bf16 = jnp.float32, jnp.bfloat16
    onehot = expert_ids[:, :, None] == jnp.arange(expert_count, dtype=jnp.int32)
    named = jnp.sum(onehot.astype(f32), axis=1)
    weights = jnp.sum(
        jnp.where(onehot, (gate_codes.astype(f32) / 65536.0)[:, :, None], 0.0), axis=1
    )
    before = jnp.arange(rows)[:, None] >= jnp.arange(rows)[None, :]
    counts = jnp.sum(jnp.where(before[:, :, None], named[None, :, :], 0.0), axis=1)
    ranks = jnp.where(named > 0, counts - 1.0, -1.0)
    table = jnp.concatenate([ranks, weights], axis=1)
    flat = jnp.pad(table, ((0, 0), (0, LANES - 2 * expert_count)))
    turned = jnp.pad(table.T, ((0, 0), (0, LANES - rows)))
    meta = jnp.concatenate([flat, turned], axis=0)
    group = 2 * capacity
    vm = pltpu.VMEM
    pairs = [pltpu.SemaphoreType.DMA((depth,))] * 18
    return pl.pallas_call(
        functools.partial(fused, depth, expert_count, capacity),
        out_shape=jax.ShapeDtypeStruct((rows, width), bf16),
        in_specs=[pl.BlockSpec(memory_space=pltpu.VMEM)] * 2
        + [pl.BlockSpec(memory_space=pl.ANY)] * 3,
        out_specs=pl.BlockSpec(memory_space=pltpu.VMEM),
        scratch_shapes=[
            vm((depth, rows, width), bf16),
            vm((depth,) + meta.shape, f32),
            vm((depth, capacity, width), bf16),
            vm((depth, 4 * group, width), bf16),
            vm(w_gate.shape[1:], bf16),
            vm(w_up.shape[1:], bf16),
            vm(w_down.shape[1:], bf16),
            vm((4 * group, part_width), bf16),
            vm((depth, 4 * group, width), bf16),
            vm((depth, 2 * group, width), bf16),
            vm((depth, group, width), bf16),
            vm((depth, group, width), bf16),
            vm((depth, group, width), bf16),
            vm((depth, capacity, width), bf16),
            vm((depth, rows, width), bf16),
            vm((depth, rows, width), bf16),
            vm((rows, width), f32),
            pltpu.SemaphoreType.DMA((3,)),
        ] + pairs,
        compiler_params=pltpu.CompilerParams(
            collective_id=0, has_side_effects=True, vmem_limit_bytes=63 << 20
        ),
    )(tokens, meta, w_gate, w_up, w_down)


def slot_plan(tokens, expert_ids, gate_codes, w_gate, w_up, w_down):
    tok_rows, top_count = expert_ids.shape
    width = tokens.shape[1]
    expert_count = lax.axis_size("expert") * w_gate.shape[0]
    capacity = 3 * tok_rows * top_count // (2 * expert_count)
    slot_count = expert_count * capacity
    flat_ids = expert_ids.reshape(-1)
    onehot = (flat_ids[:, None] == jnp.arange(expert_count, dtype=jnp.int32)[None, :]).astype(
        jnp.int32
    )
    ranking = jnp.sum((jnp.cumsum(onehot, axis=0) - 1) * onehot, axis=1)
    target = flat_ids * capacity + ranking
    picker = (target[:, None] == jnp.arange(slot_count, dtype=jnp.int32)[None, :]).astype(
        jnp.bfloat16
    )
    selector = jnp.sum(picker.reshape(tok_rows, top_count, slot_count), axis=1)
    outgoing = jnp.einsum("ts,td->sd", selector, tokens, preferred_element_type=jnp.float32).astype(
        jnp.bfloat16
    )
    arrived = lax.all_to_all(outgoing, "expert", split_axis=0, concat_axis=0, tiled=True)
    gathered = lax.all_gather(arrived, "replica", axis=0, tiled=True)
    gate = jnp.dot(gathered, w_gate[0], preferred_element_type=jnp.float32)
    up = jnp.dot(gathered, w_up[0], preferred_element_type=jnp.float32)
    hidden = activate(gate, up).astype(jnp.bfloat16)
    summed = lax.psum_scatter(
        jnp.dot(hidden, w_down[0], preferred_element_type=jnp.float32).astype(jnp.bfloat16),
        "replica",
        scatter_dimension=0,
        tiled=True,
    )
    returned = lax.all_to_all(summed, "expert", split_axis=0, concat_axis=0, tiled=True)
    per_choice = jnp.dot(picker, returned, preferred_element_type=jnp.float32)
    gates = gate_codes.astype(jnp.float32) / 65536.0
    weighted = per_choice.reshape(tok_rows, top_count, width) * gates[:, :, None]
    return jnp.sum(weighted, axis=1).astype(jnp.bfloat16)


def on_device(tokens, expert_ids, gate_codes, w_gate, w_up, w_down):
    rows, top = expert_ids.shape
    expert_count = lax.axis_size("expert") * w_gate.shape[0]
    capacity = 3 * rows * top // (2 * expert_count)
    args = (tokens, expert_ids, gate_codes, w_gate, w_up, w_down)
    paired = w_gate.shape[0] == 1 and lax.axis_size("replica") == 2 * CORES
    if paired and 2 * capacity > rows:
        return gathered_plan(*args, capacity, expert_count)
    return slot_plan(*args)


def solution(mesh):
    return jax.shard_map(
        on_device,
        mesh=mesh,
        in_specs=(
            P(("expert", "replica"), None),
            P(("expert", "replica"), None),
            P(("expert", "replica"), None),
            P("expert", None, "replica"),
            P("expert", None, "replica"),
            P("expert", "replica", None),
        ),
        out_specs=P(("expert", "replica"), None),
        check_vma=False,
    )
```

```python
import functools

import jax
import jax.numpy as jnp
from jax import lax
from jax.experimental import pallas as pl
from jax.experimental.pallas import tpu as pltpu
from jax.sharding import PartitionSpec as P

MESH = pl.DeviceIdType.MESH
CORES = 2
LANES = 128


def activate(gate, up):
    return gate * jax.nn.sigmoid(1.702 * gate) * (up + 1.0)


def spans(extent, step):
    return [(low, min(low + step, extent)) for low in range(0, extent, step)]


def fused(
    depth, experts, cap, tokens, meta, w_gate, w_up, w_down, out,
    tok_buf, meta_buf, y_out, x_buf, wg, wu, wd, hid, part, c_in, x_out, x_in,
    mine, y_in, z_out, z_in, acc, w_sem,
    zt_s, zt_r, zm_s, zm_r, y_s, y_r, xa_s, xa_r, xb_s, xb_r, c_s, c_r,
    pc_s, pc_r, pa_s, pa_r, pb_s, pb_r, py_s, py_r, pz_s, pz_r,
):
    rows, width = tokens.shape
    f32, bf16 = jnp.float32, jnp.bfloat16
    expert, replica = lax.axis_index("expert"), lax.axis_index("replica")
    z, y = expert // 2, expert % 2
    other = z * 2 + (1 - y)
    y_peer = {"expert": other}
    x_peer = {"replica": (replica + CORES) % (2 * CORES)}
    c_peer = {"replica": replica // CORES * CORES + (1 - replica % CORES)}

    def z_peer(back):
        return {"expert": ((z + depth - back) % depth) * 2 + y}

    def z_ahead(ahead):
        return {"expert": ((z + ahead) % depth) * 2 + y}

    def send(src, dst, ssem, rsem, peer):
        pltpu.make_async_remote_copy(
            src_ref=src, dst_ref=dst, send_sem=ssem, recv_sem=rsem,
            device_id=peer, device_id_type=MESH,
        ).start()

    def arrived(dst, sem):
        pltpu.make_async_copy(dst, dst, sem).wait()

    barrier = pltpu.get_barrier_semaphore()
    for peer in [z_peer(s) for s in range(1, depth)] + [y_peer, x_peer, c_peer]:
        pl.semaphore_signal(barrier, inc=1, device_id=peer, device_id_type=MESH)
    pl.semaphore_wait(barrier, depth + 2)

    for s in range(1, depth):
        send(meta, meta_buf.at[s], zm_s.at[s], zm_r.at[s], z_peer(s))
        send(tokens, tok_buf.at[s], zt_s.at[s], zt_r.at[s], z_peer(s))
    pltpu.make_async_copy(meta, meta_buf.at[0], zm_r.at[0]).start()
    pltpu.make_async_copy(tokens, tok_buf.at[0], zt_r.at[0]).start()
    loads = [
        pltpu.make_async_copy(src.at[0], dst, w_sem.at[i])
        for i, (src, dst) in enumerate(((w_gate, wg), (w_up, wu), (w_down, wd)))
    ]
    for load in loads:
        load.start()

    group = 2 * cap

    def pick(s, which):
        ranks = meta_buf[s, pl.ds(rows, 2 * experts), :]
        sub = lax.broadcasted_iota(jnp.int32, ranks.shape, 0)
        rank = jnp.sum(jnp.where(sub == which, ranks, 0.0), axis=0, keepdims=True)[:, :rows]
        slot = lax.broadcasted_iota(jnp.int32, (cap, rows), 0).astype(f32)
        return jnp.where(slot == rank, 1.0, 0.0).astype(bf16)

    def spread(s, which):
        ranks = meta_buf[s, pl.ds(0, rows), :]
        lane = lax.broadcasted_iota(jnp.int32, ranks.shape, 1)
        rank = jnp.sum(jnp.where(lane == which, ranks, 0.0), axis=1, keepdims=True)
        weight = jnp.sum(jnp.where(lane == which + experts, ranks, 0.0), axis=1, keepdims=True)
        slot = lax.broadcasted_iota(jnp.int32, (rows, cap), 1).astype(f32)
        return jnp.where(slot == rank, 1.0, 0.0).astype(bf16), weight

    def choose(s):
        arrived(meta_buf.at[s], zm_r.at[s])
        arrived(tok_buf.at[s], zt_r.at[s])
        block = tok_buf[s]
        y_out[s] = jnp.dot(pick(s, other), block, preferred_element_type=f32).astype(bf16)
        send(y_out.at[s], x_buf.at[s, pl.ds(cap, cap)], y_s.at[s], y_r.at[s], y_peer)
        x_buf[s, pl.ds(0, cap), :] = jnp.dot(
            pick(s, expert), block, preferred_element_type=f32
        ).astype(bf16)
        send(x_buf.at[s, pl.ds(0, cap)], x_buf.at[s, pl.ds(group, cap)],
             xa_s.at[s], xa_r.at[s], x_peer)

    def to_x(s):
        arrived(y_out.at[s], y_r.at[s])
        send(x_buf.at[s, pl.ds(cap, cap)], x_buf.at[s, pl.ds(group + cap, cap)],
             xb_s.at[s], xb_r.at[s], x_peer)

    def to_core(s):
        arrived(y_out.at[s], xa_r.at[s])
        arrived(y_out.at[s], xb_r.at[s])
        send(x_buf.at[s, pl.ds(0, 2 * group)], x_buf.at[s, pl.ds(2 * group, 2 * group)],
             c_s.at[s], c_r.at[s], c_peer)

    def ffn(s):
        arrived(c_in.at[s], c_r.at[s])

        @pl.when(s == 0)
        def _():
            for load in loads:
                load.wait()

        across = (((1,), (1,)), ((), ()))
        for low, high in spans(wg.shape[0], 256):
            block = x_buf[s]
            gate = lax.dot_general(block, wg[low:high, :], across, preferred_element_type=f32)
            up = lax.dot_general(block, wu[low:high, :], across, preferred_element_type=f32)
            hid[:, low:high] = activate(gate, up).astype(bf16)
        for low, high in spans(width, 512):
            part[s, :, low:high] = jnp.dot(
                hid[...], wd[:, low:high], preferred_element_type=f32
            ).astype(bf16)
        send(part.at[s, pl.ds(2 * group, 2 * group)], c_in.at[s], pc_s.at[s], pc_r.at[s], c_peer)

    def turn(i):
        return (i + 1) % depth

    def sum_core(i):
        s = turn(i)
        arrived(c_in.at[s], pc_r.at[s])
        for low, ssem, rsem in ((cap, pa_s, pa_r), (0, pb_s, pb_r)):
            x_out[s, pl.ds(low, cap), :] = (
                part[s, pl.ds(group + low, cap), :].astype(f32)
                + c_in[s, pl.ds(group + low, cap), :].astype(f32)
            ).astype(bf16)
            send(x_out.at[s, pl.ds(low, cap)], x_in.at[s, pl.ds(low, cap)],
                 ssem.at[s], rsem.at[s], x_peer)

    def add_up(s, low, rsem):
        arrived(y_in.at[s], rsem.at[s])
        mine[s, pl.ds(low, cap), :] = (
            part[s, pl.ds(low, cap), :].astype(f32)
            + c_in[s, pl.ds(low, cap), :].astype(f32)
            + x_in[s, pl.ds(low, cap), :].astype(f32)
        ).astype(bf16)

    def sum_x(i):
        s = turn(i)
        add_up(s, cap, pa_r)
        send(mine.at[s, pl.ds(cap, cap)], y_in.at[s], py_s.at[s], py_r.at[s], y_peer)
        add_up(s, 0, pb_r)

    def combine(i):
        s = turn(i)
        arrived(y_in.at[s], py_r.at[s])
        own_spread, own_weight = spread(s, expert)
        far_spread, far_weight = spread(s, other)
        total = own_weight * jnp.dot(
            own_spread, mine[s, pl.ds(0, cap), :], preferred_element_type=f32
        ) + far_weight * jnp.dot(far_spread, y_in[s], preferred_element_type=f32)

        @pl.when(s == 0)
        def _():
            acc[...] = total

        @pl.when(s > 0)
        def _():
            z_out[s] = total.astype(bf16)
            send(z_out.at[s], z_in.at[s], pz_s.at[s], pz_r.at[s], z_ahead(s))

    steps = ((choose, 0), (to_core, 1), (to_x, 0), (sum_core, 4), (ffn, 2), (sum_x, 5), (combine, 6))

    def tick(t, carry):
        for step, lag in steps:
            @pl.when((t >= lag) & (t < depth + lag))
            def _():
                step(t - lag)
        return carry

    lax.fori_loop(0, depth + steps[-1][1], tick, 0)

    total = acc[...]
    for s in range(1, depth):
        arrived(z_in.at[s], pz_r.at[s])
        total = total + z_in[s].astype(f32)
    out[...] = total.astype(bf16)
    for s in range(depth):
        if s:
            arrived(meta_buf.at[s], zm_s.at[s])
            arrived(tok_buf.at[s], zt_s.at[s])
            arrived(z_out.at[s], pz_s.at[s])
        arrived(y_out.at[s], y_s.at[s])
        arrived(c_in.at[s], c_s.at[s])
        arrived(c_in.at[s], pc_s.at[s])
        for sem in (xa_s, xb_s, pa_s, pb_s, py_s):
            arrived(y_in.at[s], sem.at[s])


def gathered_plan(tokens, expert_ids, gate_codes, w_gate, w_up, w_down, capacity, expert_count):
    rows, top = expert_ids.shape
    width = tokens.shape[1]
    w_gate, w_up = jnp.swapaxes(w_gate, 1, 2), jnp.swapaxes(w_up, 1, 2)
    part_width = w_gate.shape[1]
    depth = lax.axis_size("expert") // 2
    f32, bf16 = jnp.float32, jnp.bfloat16
    onehot = expert_ids[:, :, None] == jnp.arange(expert_count, dtype=jnp.int32)
    named = jnp.sum(onehot.astype(f32), axis=1)
    weights = jnp.sum(
        jnp.where(onehot, (gate_codes.astype(f32) / 65536.0)[:, :, None], 0.0), axis=1
    )
    before = jnp.arange(rows)[:, None] >= jnp.arange(rows)[None, :]
    counts = jnp.sum(jnp.where(before[:, :, None], named[None, :, :], 0.0), axis=1)
    ranks = jnp.where(named > 0, counts - 1.0, -1.0)
    table = jnp.concatenate([ranks, weights], axis=1)
    flat = jnp.pad(table, ((0, 0), (0, LANES - 2 * expert_count)))
    turned = jnp.pad(table.T, ((0, 0), (0, LANES - rows)))
    meta = jnp.concatenate([flat, turned], axis=0)
    group = 2 * capacity
    vm = pltpu.VMEM
    pairs = [pltpu.SemaphoreType.DMA((depth,))] * 22
    return pl.pallas_call(
        functools.partial(fused, depth, expert_count, capacity),
        out_shape=jax.ShapeDtypeStruct((rows, width), bf16),
        in_specs=[pl.BlockSpec(memory_space=pltpu.VMEM)] * 2
        + [pl.BlockSpec(memory_space=pl.ANY)] * 3,
        out_specs=pl.BlockSpec(memory_space=pltpu.VMEM),
        scratch_shapes=[
            vm((depth, rows, width), bf16),
            vm((depth,) + meta.shape, f32),
            vm((depth, capacity, width), bf16),
            vm((depth, 4 * group, width), bf16),
            vm(w_gate.shape[1:], bf16),
            vm(w_up.shape[1:], bf16),
            vm(w_down.shape[1:], bf16),
            vm((4 * group, part_width), bf16),
            vm((depth, 4 * group, width), bf16),
            vm((depth, 2 * group, width), bf16),
            vm((depth, group, width), bf16),
            vm((depth, group, width), bf16),
            vm((depth, group, width), bf16),
            vm((depth, capacity, width), bf16),
            vm((depth, rows, width), bf16),
            vm((depth, rows, width), bf16),
            vm((rows, width), f32),
            pltpu.SemaphoreType.DMA((3,)),
        ] + pairs,
        compiler_params=pltpu.CompilerParams(
            collective_id=0, has_side_effects=True, vmem_limit_bytes=63 << 20
        ),
    )(tokens, meta, w_gate, w_up, w_down)


def slot_plan(tokens, expert_ids, gate_codes, w_gate, w_up, w_down):
    tok_rows, top_count = expert_ids.shape
    width = tokens.shape[1]
    expert_count = lax.axis_size("expert") * w_gate.shape[0]
    capacity = 3 * tok_rows * top_count // (2 * expert_count)
    slot_count = expert_count * capacity
    flat_ids = expert_ids.reshape(-1)
    onehot = (flat_ids[:, None] == jnp.arange(expert_count, dtype=jnp.int32)[None, :]).astype(
        jnp.int32
    )
    ranking = jnp.sum((jnp.cumsum(onehot, axis=0) - 1) * onehot, axis=1)
    target = flat_ids * capacity + ranking
    picker = (target[:, None] == jnp.arange(slot_count, dtype=jnp.int32)[None, :]).astype(
        jnp.bfloat16
    )
    selector = jnp.sum(picker.reshape(tok_rows, top_count, slot_count), axis=1)
    outgoing = jnp.einsum("ts,td->sd", selector, tokens, preferred_element_type=jnp.float32).astype(
        jnp.bfloat16
    )
    arrived = lax.all_to_all(outgoing, "expert", split_axis=0, concat_axis=0, tiled=True)
    gathered = lax.all_gather(arrived, "replica", axis=0, tiled=True)
    gate = jnp.dot(gathered, w_gate[0], preferred_element_type=jnp.float32)
    up = jnp.dot(gathered, w_up[0], preferred_element_type=jnp.float32)
    hidden = activate(gate, up).astype(jnp.bfloat16)
    summed = lax.psum_scatter(
        jnp.dot(hidden, w_down[0], preferred_element_type=jnp.float32).astype(jnp.bfloat16),
        "replica",
        scatter_dimension=0,
        tiled=True,
    )
    returned = lax.all_to_all(summed, "expert", split_axis=0, concat_axis=0, tiled=True)
    per_choice = jnp.dot(picker, returned, preferred_element_type=jnp.float32)
    gates = gate_codes.astype(jnp.float32) / 65536.0
    weighted = per_choice.reshape(tok_rows, top_count, width) * gates[:, :, None]
    return jnp.sum(weighted, axis=1).astype(jnp.bfloat16)


def on_device(tokens, expert_ids, gate_codes, w_gate, w_up, w_down):
    rows, top = expert_ids.shape
    expert_count = lax.axis_size("expert") * w_gate.shape[0]
    capacity = 3 * rows * top // (2 * expert_count)
    args = (tokens, expert_ids, gate_codes, w_gate, w_up, w_down)
    paired = w_gate.shape[0] == 1 and lax.axis_size("replica") == 2 * CORES
    if paired and 2 * capacity > rows:
        return gathered_plan(*args, capacity, expert_count)
    return slot_plan(*args)


def solution(mesh):
    return jax.shard_map(
        on_device,
        mesh=mesh,
        in_specs=(
            P(("expert", "replica"), None),
            P(("expert", "replica"), None),
            P(("expert", "replica"), None),
            P("expert", None, "replica"),
            P("expert", None, "replica"),
            P("expert", "replica", None),
        ),
        out_specs=P(("expert", "replica"), None),
        check_vma=False,
    )
```

```python
import functools

import jax
import jax.numpy as jnp
from jax import lax
from jax.experimental import pallas as pl
from jax.experimental.pallas import tpu as pltpu
from jax.sharding import PartitionSpec as P

MESH = pl.DeviceIdType.MESH
CORES = 2
LANES = 128


def activate(gate, up):
    return gate * jax.nn.sigmoid(1.702 * gate) * (up + 1.0)


def spans(extent, step):
    return [(low, min(low + step, extent)) for low in range(0, extent, step)]


def stage_hops(depth):
    middle = depth // 2
    return [0, middle] + [s for s in range(1, depth) if s != middle]


def fused(
    depth, experts, cap, tokens, meta, w_gate, w_up, w_down, out,
    tok_buf, meta_buf, y_out, x_buf, wg, wu, wd, hid, part, c_in, x_out, x_in,
    mine, y_in, z_out, z_in, acc, w_sem,
    zt_s, zt_r, zm_s, zm_r, y_s, y_r, xa_s, xa_r, xb_s, xb_r, c_s, c_r,
    pc_s, pc_r, pa_s, pa_r, pb_s, pb_r, py_s, py_r, pz_s, pz_r,
):
    rows, width = tokens.shape
    f32, bf16 = jnp.float32, jnp.bfloat16
    expert, replica = lax.axis_index("expert"), lax.axis_index("replica")
    z, y = expert // 2, expert % 2
    other = z * 2 + (1 - y)
    y_peer = {"expert": other}
    x_peer = {"replica": (replica + CORES) % (2 * CORES)}
    c_peer = {"replica": replica // CORES * CORES + (1 - replica % CORES)}

    def z_peer(back):
        return {"expert": ((z + depth - back) % depth) * 2 + y}

    def z_ahead(ahead):
        return {"expert": ((z + ahead) % depth) * 2 + y}

    def send(src, dst, ssem, rsem, peer):
        pltpu.make_async_remote_copy(
            src_ref=src, dst_ref=dst, send_sem=ssem, recv_sem=rsem,
            device_id=peer, device_id_type=MESH,
        ).start()

    def arrived(dst, sem):
        pltpu.make_async_copy(dst, dst, sem).wait()

    barrier = pltpu.get_barrier_semaphore()
    for peer in [z_peer(s) for s in range(1, depth)] + [y_peer, x_peer, c_peer]:
        pl.semaphore_signal(barrier, inc=1, device_id=peer, device_id_type=MESH)
    pl.semaphore_wait(barrier, depth + 2)

    hops = stage_hops(depth)
    for s in range(1, depth):
        send(meta, meta_buf.at[s], zm_s.at[s], zm_r.at[s], z_peer(hops[s]))
        send(tokens, tok_buf.at[s], zt_s.at[s], zt_r.at[s], z_peer(hops[s]))
    pltpu.make_async_copy(meta, meta_buf.at[0], zm_r.at[0]).start()
    pltpu.make_async_copy(tokens, tok_buf.at[0], zt_r.at[0]).start()
    loads = [
        pltpu.make_async_copy(src.at[0], dst, w_sem.at[i])
        for i, (src, dst) in enumerate(((w_gate, wg), (w_up, wu), (w_down, wd)))
    ]
    for load in loads:
        load.start()

    group = 2 * cap

    def pick(s, which):
        ranks = meta_buf[s, pl.ds(rows, 2 * experts), :]
        sub = lax.broadcasted_iota(jnp.int32, ranks.shape, 0)
        rank = jnp.sum(jnp.where(sub == which, ranks, 0.0), axis=0, keepdims=True)[:, :rows]
        slot = lax.broadcasted_iota(jnp.int32, (cap, rows), 0).astype(f32)
        return jnp.where(slot == rank, 1.0, 0.0).astype(bf16)

    def spread(s, which):
        ranks = meta_buf[s, pl.ds(0, rows), :]
        lane = lax.broadcasted_iota(jnp.int32, ranks.shape, 1)
        rank = jnp.sum(jnp.where(lane == which, ranks, 0.0), axis=1, keepdims=True)
        weight = jnp.sum(jnp.where(lane == which + experts, ranks, 0.0), axis=1, keepdims=True)
        slot = lax.broadcasted_iota(jnp.int32, (rows, cap), 1).astype(f32)
        return jnp.where(slot == rank, 1.0, 0.0).astype(bf16), weight

    def choose(s):
        arrived(meta_buf.at[s], zm_r.at[s])
        arrived(tok_buf.at[s], zt_r.at[s])
        block = tok_buf[s]
        y_out[s] = jnp.dot(pick(s, other), block, preferred_element_type=f32).astype(bf16)
        send(y_out.at[s], x_buf.at[s, pl.ds(cap, cap)], y_s.at[s], y_r.at[s], y_peer)
        x_buf[s, pl.ds(0, cap), :] = jnp.dot(
            pick(s, expert), block, preferred_element_type=f32
        ).astype(bf16)
        send(x_buf.at[s, pl.ds(0, cap)], x_buf.at[s, pl.ds(group, cap)],
             xa_s.at[s], xa_r.at[s], x_peer)

    def to_x(s):
        arrived(y_out.at[s], y_r.at[s])
        send(x_buf.at[s, pl.ds(cap, cap)], x_buf.at[s, pl.ds(group + cap, cap)],
             xb_s.at[s], xb_r.at[s], x_peer)

    def to_core(s):
        arrived(y_out.at[s], xa_r.at[s])
        arrived(y_out.at[s], xb_r.at[s])
        send(x_buf.at[s, pl.ds(0, 2 * group)], x_buf.at[s, pl.ds(2 * group, 2 * group)],
             c_s.at[s], c_r.at[s], c_peer)

    def ffn(s):
        arrived(c_in.at[s], c_r.at[s])

        @pl.when(s == 0)
        def _():
            for load in loads:
                load.wait()

        across = (((1,), (1,)), ((), ()))
        for low, high in spans(wg.shape[0], 256):
            block = x_buf[s]
            gate = lax.dot_general(block, wg[low:high, :], across, preferred_element_type=f32)
            up = lax.dot_general(block, wu[low:high, :], across, preferred_element_type=f32)
            hid[:, low:high] = activate(gate, up).astype(bf16)
        for low, high in spans(width, 512):
            part[s, :, low:high] = jnp.dot(
                hid[...], wd[:, low:high], preferred_element_type=f32
            ).astype(bf16)
        send(part.at[s, pl.ds(2 * group, 2 * group)], c_in.at[s], pc_s.at[s], pc_r.at[s], c_peer)

    def turn(i):
        return (i + 1) % depth

    def sum_core(i):
        s = turn(i)
        arrived(c_in.at[s], pc_r.at[s])
        for low, ssem, rsem in ((cap, pa_s, pa_r), (0, pb_s, pb_r)):
            x_out[s, pl.ds(low, cap), :] = (
                part[s, pl.ds(group + low, cap), :].astype(f32)
                + c_in[s, pl.ds(group + low, cap), :].astype(f32)
            ).astype(bf16)
            send(x_out.at[s, pl.ds(low, cap)], x_in.at[s, pl.ds(low, cap)],
                 ssem.at[s], rsem.at[s], x_peer)

    def add_up(s, low, rsem):
        arrived(y_in.at[s], rsem.at[s])
        mine[s, pl.ds(low, cap), :] = (
            part[s, pl.ds(low, cap), :].astype(f32)
            + c_in[s, pl.ds(low, cap), :].astype(f32)
            + x_in[s, pl.ds(low, cap), :].astype(f32)
        ).astype(bf16)

    def sum_x(i):
        s = turn(i)
        add_up(s, cap, pa_r)
        send(mine.at[s, pl.ds(cap, cap)], y_in.at[s], py_s.at[s], py_r.at[s], y_peer)
        add_up(s, 0, pb_r)

    def combine(i):
        s = turn(i)
        arrived(y_in.at[s], py_r.at[s])
        own_spread, own_weight = spread(s, expert)
        far_spread, far_weight = spread(s, other)
        total = own_weight * jnp.dot(
            own_spread, mine[s, pl.ds(0, cap), :], preferred_element_type=f32
        ) + far_weight * jnp.dot(far_spread, y_in[s], preferred_element_type=f32)

        @pl.when(s == 0)
        def _():
            acc[...] = total

        for k in range(1, depth):
            @pl.when(s == k)
            def _():
                z_out[k] = total.astype(bf16)
                send(z_out.at[k], z_in.at[k], pz_s.at[k], pz_r.at[k], z_ahead(hops[k]))

    steps = ((choose, 0), (to_core, 1), (to_x, 0), (sum_core, 4), (ffn, 2), (sum_x, 5), (combine, 6))

    def tick(t, carry):
        for step, lag in steps:
            @pl.when((t >= lag) & (t < depth + lag))
            def _():
                step(t - lag)
        return carry

    lax.fori_loop(0, depth + steps[-1][1], tick, 0)

    total = acc[...]
    for s in range(1, depth):
        arrived(z_in.at[s], pz_r.at[s])
        total = total + z_in[s].astype(f32)
    out[...] = total.astype(bf16)
    for s in range(depth):
        if s:
            arrived(meta_buf.at[s], zm_s.at[s])
            arrived(tok_buf.at[s], zt_s.at[s])
            arrived(z_out.at[s], pz_s.at[s])
        arrived(y_out.at[s], y_s.at[s])
        arrived(c_in.at[s], c_s.at[s])
        arrived(c_in.at[s], pc_s.at[s])
        for sem in (xa_s, xb_s, pa_s, pb_s, py_s):
            arrived(y_in.at[s], sem.at[s])


def gathered_plan(tokens, expert_ids, gate_codes, w_gate, w_up, w_down, capacity, expert_count):
    rows, top = expert_ids.shape
    width = tokens.shape[1]
    w_gate, w_up = jnp.swapaxes(w_gate, 1, 2), jnp.swapaxes(w_up, 1, 2)
    part_width = w_gate.shape[1]
    depth = lax.axis_size("expert") // 2
    f32, bf16 = jnp.float32, jnp.bfloat16
    onehot = expert_ids[:, :, None] == jnp.arange(expert_count, dtype=jnp.int32)
    named = jnp.sum(onehot.astype(f32), axis=1)
    weights = jnp.sum(
        jnp.where(onehot, (gate_codes.astype(f32) / 65536.0)[:, :, None], 0.0), axis=1
    )
    before = jnp.arange(rows)[:, None] >= jnp.arange(rows)[None, :]
    counts = jnp.sum(jnp.where(before[:, :, None], named[None, :, :], 0.0), axis=1)
    ranks = jnp.where(named > 0, counts - 1.0, -1.0)
    table = jnp.concatenate([ranks, weights], axis=1)
    flat = jnp.pad(table, ((0, 0), (0, LANES - 2 * expert_count)))
    turned = jnp.pad(table.T, ((0, 0), (0, LANES - rows)))
    meta = jnp.concatenate([flat, turned], axis=0)
    group = 2 * capacity
    vm = pltpu.VMEM
    pairs = [pltpu.SemaphoreType.DMA((depth,))] * 22
    return pl.pallas_call(
        functools.partial(fused, depth, expert_count, capacity),
        out_shape=jax.ShapeDtypeStruct((rows, width), bf16),
        in_specs=[pl.BlockSpec(memory_space=pltpu.VMEM)] * 2
        + [pl.BlockSpec(memory_space=pl.ANY)] * 3,
        out_specs=pl.BlockSpec(memory_space=pltpu.VMEM),
        scratch_shapes=[
            vm((depth, rows, width), bf16),
            vm((depth,) + meta.shape, f32),
            vm((depth, capacity, width), bf16),
            vm((depth, 4 * group, width), bf16),
            vm(w_gate.shape[1:], bf16),
            vm(w_up.shape[1:], bf16),
            vm(w_down.shape[1:], bf16),
            vm((4 * group, part_width), bf16),
            vm((depth, 4 * group, width), bf16),
            vm((depth, 2 * group, width), bf16),
            vm((depth, group, width), bf16),
            vm((depth, group, width), bf16),
            vm((depth, group, width), bf16),
            vm((depth, capacity, width), bf16),
            vm((depth, rows, width), bf16),
            vm((depth, rows, width), bf16),
            vm((rows, width), f32),
            pltpu.SemaphoreType.DMA((3,)),
        ] + pairs,
        compiler_params=pltpu.CompilerParams(
            collective_id=0, has_side_effects=True, vmem_limit_bytes=63 << 20
        ),
    )(tokens, meta, w_gate, w_up, w_down)


def slot_plan(tokens, expert_ids, gate_codes, w_gate, w_up, w_down):
    tok_rows, top_count = expert_ids.shape
    width = tokens.shape[1]
    expert_count = lax.axis_size("expert") * w_gate.shape[0]
    capacity = 3 * tok_rows * top_count // (2 * expert_count)
    slot_count = expert_count * capacity
    flat_ids = expert_ids.reshape(-1)
    onehot = (flat_ids[:, None] == jnp.arange(expert_count, dtype=jnp.int32)[None, :]).astype(
        jnp.int32
    )
    ranking = jnp.sum((jnp.cumsum(onehot, axis=0) - 1) * onehot, axis=1)
    target = flat_ids * capacity + ranking
    picker = (target[:, None] == jnp.arange(slot_count, dtype=jnp.int32)[None, :]).astype(
        jnp.bfloat16
    )
    selector = jnp.sum(picker.reshape(tok_rows, top_count, slot_count), axis=1)
    outgoing = jnp.einsum("ts,td->sd", selector, tokens, preferred_element_type=jnp.float32).astype(
        jnp.bfloat16
    )
    arrived = lax.all_to_all(outgoing, "expert", split_axis=0, concat_axis=0, tiled=True)
    gathered = lax.all_gather(arrived, "replica", axis=0, tiled=True)
    gate = jnp.dot(gathered, w_gate[0], preferred_element_type=jnp.float32)
    up = jnp.dot(gathered, w_up[0], preferred_element_type=jnp.float32)
    hidden = activate(gate, up).astype(jnp.bfloat16)
    summed = lax.psum_scatter(
        jnp.dot(hidden, w_down[0], preferred_element_type=jnp.float32).astype(jnp.bfloat16),
        "replica",
        scatter_dimension=0,
        tiled=True,
    )
    returned = lax.all_to_all(summed, "expert", split_axis=0, concat_axis=0, tiled=True)
    per_choice = jnp.dot(picker, returned, preferred_element_type=jnp.float32)
    gates = gate_codes.astype(jnp.float32) / 65536.0
    weighted = per_choice.reshape(tok_rows, top_count, width) * gates[:, :, None]
    return jnp.sum(weighted, axis=1).astype(jnp.bfloat16)


def on_device(tokens, expert_ids, gate_codes, w_gate, w_up, w_down):
    rows, top = expert_ids.shape
    expert_count = lax.axis_size("expert") * w_gate.shape[0]
    capacity = 3 * rows * top // (2 * expert_count)
    args = (tokens, expert_ids, gate_codes, w_gate, w_up, w_down)
    paired = w_gate.shape[0] == 1 and lax.axis_size("replica") == 2 * CORES
    if paired and 2 * capacity > rows:
        return gathered_plan(*args, capacity, expert_count)
    return slot_plan(*args)


def solution(mesh):
    return jax.shard_map(
        on_device,
        mesh=mesh,
        in_specs=(
            P(("expert", "replica"), None),
            P(("expert", "replica"), None),
            P(("expert", "replica"), None),
            P("expert", None, "replica"),
            P("expert", None, "replica"),
            P("expert", "replica", None),
        ),
        out_specs=P(("expert", "replica"), None),
        check_vma=False,
    )
```
